32 devices in a mesh: seq: 8 (over z, y), ch: 4 (over x, core).
Axes of the slice: x: 2, y: 2, z: 4, core: 2. Of those that a mesh axis runs over, the one named last changes fastest.
Arguments:
- hidden_in: bfloat16 [4096, 1024], P('seq'), may hold values from -6 to 6
- proj_zx: bfloat16 [512, 2, 1024], P(None, None, 'ch'), may hold values from -0.25 to 0.25
- proj_bc: bfloat16 [512, 128], replicated, may hold values from -0.0625 to 0.0625
- proj_dt: bfloat16 [512, 16], P(None, 'ch'), may hold values from -0.25 to 0.25
- conv_x: bfloat16 [4, 1024], P(None, 'ch'), may hold values from -3 to 3
- conv_bc: bfloat16 [4, 128], replicated, may hold values from -3 to 3
- dt_bias: float32 [16], P('ch'), may hold values from -7 to 1, as said below
- decay_exp: int32 [16], P('ch'), may hold values from 2 to 25
- skip_gain: float32 [16], P('ch'), may hold values from 0.5 to 1.5
- norm_gain: float32 [1024], P('ch'), may hold values from 0.5 to 2
- out_proj: bfloat16 [1024, 512], P('ch'), may hold values from -0.1875 to 0.1875
Outputs:
- hidden_out: bfloat16 [4096, 1024], P('seq', 'ch')
The draws below stay inside these ranges and needn't reach their ends.
Inputs may be any that keep to these rules, and one draw needn't show every extreme that they name: `dt_bias`: added to each head's step size logits before the softplus.
All inputs are finite; a program needn't handle non-finite values.
Results may differ from the reference program's by a relative error of at most 0.013.
Values may be sent and summed in bfloat16 or wider, within the bound.
A program may use at most 128 MiB of HBM per device.

```python
import jax
import jax.numpy as jnp
from jax import lax

D = 512
INNER = 1024
HEADS = 16
STATE = 64
KERNEL = 4
BLOCK = 256
HEADP = 64
TOKENS = 4096


def draw_dt_bias(key, part):
    return jax.random.uniform(key, (HEADS,), jnp.float32, -2.0, 1.0)


def plant(values, rng, smallest, largest):
    shape = values.shape
    index_at = [jax.random.randint(jax.random.fold_in(rng, axis), (), 0, shape[axis]) for axis in range(len(shape))]
    values = values.at[tuple(index_at)].set(smallest)
    longest = shape.index(max(shape))
    index_at[longest] = (index_at[longest] + 1) % shape[longest]
    return values.at[tuple(index_at)].set(largest)


def steps_of(rng, extent, shards, smallest, high):
    factor_of, own = 1.0, jax.random.fold_in(rng, 6)
    for dim, parts in shards:
        steps = jnp.exp(jax.random.uniform(jax.random.fold_in(own, dim), (parts,), jnp.float32, smallest / len(shards), high / len(shards)))
        factor_of = factor_of * jnp.repeat(steps, extent[dim] // parts).reshape([-1 if axis == dim else 1 for axis in range(len(extent))])
    return factor_of


def centred(stream_key, shape, spread, bound, cuts=(), held_as=jnp.bfloat16):
    values = jax.random.normal(stream_key, shape, jnp.float32) * spread
    if len(cuts) > 0:
        values = steps_of(stream_key, shape, cuts, -0.22, 0.18) * values
    return jnp.clip(values, min=-bound, max=bound).astype(held_as)


def setup_inputs(seed: int = 0) -> dict:
    key_list = jax.random.split(jax.random.key(seed), 12)
    hidden_in = centred(key_list[0], (TOKENS, 2 * D), 1.0, 6.0, ((0, 8),))
    proj_zx = centred(key_list[1], (D, 2, INNER), D ** -0.5, 0.25, ((2, 4),))
    proj_bc = centred(key_list[2], (D, 2 * STATE), (16 * D) ** -0.5, 0.0625)
    proj_dt = centred(key_list[3], (D, HEADS), D ** -0.5, 0.25, ((1, 4),))
    conv_x = centred(key_list[4], (KERNEL, INNER), KERNEL ** -0.5, 3.0, ((1, 4),))
    conv_bc = centred(key_list[5], (KERNEL, 2 * STATE), KERNEL ** -0.5, 3.0)
    dt_bias = draw_dt_bias(jax.random.fold_in(key_list[11], 71), 0)
    decay_exp = plant(jax.random.randint(key_list[7], (HEADS,), 2, 26), jax.random.fold_in(key_list[7], 1), 2, 25).astype(jnp.int32)
    skip_gain = jnp.clip(0.5 + 1.0 * jax.random.uniform(key_list[8], (HEADS,), jnp.float32) ** steps_of(key_list[8], (HEADS,), ((0, 4),), -0.2, 0.2), 0.5, 1.5)
    norm_gain = jnp.clip(0.5 + 1.5 * jax.random.uniform(key_list[9], (INNER,), jnp.float32) ** steps_of(key_list[9], (INNER,), ((0, 4),), -0.2, 0.2), 0.5, 2.0)
    out_proj = centred(key_list[10], (INNER, D), INNER ** -0.5, 0.1875, ((0, 4),))
    return dict(hidden_in=hidden_in, proj_zx=proj_zx, proj_bc=proj_bc, proj_dt=proj_dt, conv_x=conv_x, conv_bc=conv_bc, dt_bias=dt_bias, decay_exp=decay_exp, skip_gain=skip_gain, norm_gain=norm_gain, out_proj=out_proj)


EPS = 1e-05

def causal_conv(padded, kernel_taps, row_count):
    accumulated = jnp.zeros((row_count, padded.shape[1]), jnp.float32)
    for offset in range(kernel_taps.shape[0]):
        accumulated = accumulated + kernel_taps[offset].astype(jnp.float32) * padded[offset:offset + row_count].astype(jnp.float32)
    return jax.nn.silu(accumulated).astype(jnp.bfloat16)

def block_step(carry_state, values, b_rows, c_rows, dt_block, ld_block, skip_gain):
    block_rows = values.shape[0]
    cumulative = jnp.cumsum(ld_block, axis=0)
    scores = jnp.dot(c_rows, b_rows.T, preferred_element_type=jnp.float32)
    differences = cumulative.T[:, :, None] - cumulative.T[:, None, :]
    positions = jnp.arange(block_rows, dtype=jnp.int32)
    causal_mask = positions[:, None] >= positions[None, :]
    decays = jnp.exp(jnp.where(causal_mask[None], differences, -jnp.inf))
    weights = (scores[None] * decays * dt_block.T[:, None, :]).astype(jnp.bfloat16)
    within = jnp.einsum('hts,shp->thp', weights.astype(jnp.float32), values.astype(jnp.float32))
    carried = jnp.exp(cumulative)[:, :, None] * jnp.einsum('tn,hpn->thp', c_rows.astype(jnp.float32), carry_state, precision=lax.Precision.HIGHEST)
    to_end = jnp.exp(cumulative[-1:] - cumulative) * dt_block
    loaded = (values.astype(jnp.float32) * to_end[:, :, None]).astype(jnp.bfloat16)
    added_state = jnp.einsum('thp,tn->hpn', loaded.astype(jnp.float32), b_rows.astype(jnp.float32))
    next_state = jnp.exp(cumulative[-1])[:, None, None] * carry_state + added_state
    result = within + carried + skip_gain[None, :, None] * values.astype(jnp.float32)
    return (next_state, result)

def local_pass(conv_out, step_size, log_decay, skip_gain, head_count, head_size, state_size):
    row_count = conv_out.shape[0]
    inner_width = head_count * head_size
    blocks = row_count // BLOCK
    values = conv_out[:, :inner_width].reshape(blocks, BLOCK, head_count, head_size)
    b_rows = conv_out[:, inner_width:inner_width + state_size].reshape(blocks, BLOCK, state_size)
    c_rows = conv_out[:, inner_width + state_size:].reshape(blocks, BLOCK, state_size)
    dt_blocks = step_size.reshape(blocks, BLOCK, head_count)
    ld_blocks = log_decay.reshape(blocks, BLOCK, head_count)

    def advance(carry_state, inputs):
        return block_step(carry_state, inputs[0], inputs[1], inputs[2], inputs[3], inputs[4], skip_gain)
    start_state = jnp.zeros((head_count, head_size, state_size), jnp.float32)
    final_state, outputs = lax.scan(advance, start_state, (values, b_rows, c_rows, dt_blocks, ld_blocks))
    return (outputs.reshape(row_count, head_count, head_size), final_state)

def gate_norm(mixer_out, gate_z, norm_gain):
    row_count, head_count, head_size = mixer_out.shape
    gated_out = mixer_out * jax.nn.silu(gate_z.astype(jnp.float32)).reshape(row_count, head_count, head_size)
    mean_square = lax.optimization_barrier(jnp.mean(gated_out * gated_out, axis=2, keepdims=True))
    return (gated_out * lax.rsqrt(mean_square + EPS)).reshape(row_count, head_count * head_size) * norm_gain

def strand_mix(inputs, all_weights, kernel_taps, dt_bias, decay_rate, skip_gain, norm_gain):
    projected = jnp.dot(inputs, all_weights, preferred_element_type=jnp.float32)
    gate_z = projected[:, :INNER].astype(jnp.bfloat16)
    conv_input = projected[:, INNER:2 * INNER + 2 * STATE].astype(jnp.bfloat16)
    step_size = jax.nn.softplus(projected[:, 2 * INNER + 2 * STATE:] + dt_bias)
    log_decay = -step_size * decay_rate
    padded = jnp.pad(conv_input, ((KERNEL - 1, KERNEL - 1), (0, 0)))
    ahead_conv = causal_conv(padded, kernel_taps, TOKENS)
    behind_conv = causal_conv(padded[::-1], kernel_taps, TOKENS)
    ahead_out, _ = local_pass(ahead_conv, step_size, log_decay, skip_gain, HEADS, HEADP, STATE)
    behind_out, _ = local_pass(behind_conv, step_size[::-1], log_decay[::-1], skip_gain, HEADS, HEADP, STATE)
    behind_out = behind_out[::-1]
    combined = gate_norm(ahead_out, gate_z, norm_gain) + gate_norm(behind_out, gate_z, norm_gain)
    return combined.astype(jnp.bfloat16)

def reference(hidden_in, proj_zx, proj_bc, proj_dt, conv_x, conv_bc, dt_bias, decay_exp, skip_gain, norm_gain, out_proj):
    forward_in = hidden_in[:, :D]
    reverse_in = hidden_in[:, D:][::-1, ::-1]
    all_weights = jnp.concatenate([proj_zx[:, 0, :], proj_zx[:, 1, :], proj_bc, proj_dt], axis=1)
    kernel_taps = jnp.concatenate([conv_x, conv_bc], axis=1)
    decay_rate = jnp.exp2(-decay_exp.astype(jnp.float32))
    mixed_forward = strand_mix(forward_in, all_weights, kernel_taps, dt_bias, decay_rate, skip_gain, norm_gain)
    mixed_reverse = strand_mix(reverse_in, all_weights, kernel_taps, dt_bias, decay_rate, skip_gain, norm_gain)[::-1]
    branch_forward = jnp.dot(mixed_forward, out_proj, preferred_element_type=jnp.float32)
    branch_reverse = jnp.dot(mixed_reverse, out_proj, preferred_element_type=jnp.float32)[:, ::-1]
    branch = jnp.concatenate([branch_forward, branch_reverse], axis=1)
    return (hidden_in.astype(jnp.float32) + branch).astype(jnp.bfloat16)
```

```python
import functools

import jax
import jax.numpy as jnp
from jax import lax
from jax.experimental import pallas as pl
from jax.experimental.pallas import tpu as pltpu
from jax.sharding import PartitionSpec as P

EPS = 1e-05
CHUNK = 128
HALO = 16
F32 = jnp.float32
BF16 = jnp.bfloat16
MESH = pl.DeviceIdType.MESH


def mm(a, b):
    return jnp.dot(a, b, preferred_element_type=F32)


def mm_nt(a, b):
    return lax.dot_general(a, b, (((1,), (1,)), ((), ())), preferred_element_type=F32)


def silu(v):
    half = 0.5 * v
    return half + half * jnp.tanh(half)


def reversal(size):
    row = lax.broadcasted_iota(jnp.int32, (size, size), 0)
    col = lax.broadcasted_iota(jnp.int32, (size, size), 1)
    return jnp.where(row + col == size - 1, 1.0, 0.0).astype(BF16)


def kernel(
    n_seq, n_ch, heads, taps_count,
    hid, wts, taps, par, outp, out,
    halo_lo, halo_hi, xbc, gate, step, xs, xdt, bc, cum, sadd, sent, sfin, tot, y,
    st_out, tt_out, st_in, tt_in, wout, wrev, mixed, gath,
    h_send, h_recv, w_send, w_recv, s_send, s_recv, t_send, t_recv, m_send, m_recv,
):
    rows, two_width = hid.shape
    width = two_width // 2
    inner = par.shape[1]
    bcw = wts.shape[1] - 3 * inner
    state = bcw // 2
    hp = inner // heads
    conv = inner + bcw
    chunks = rows // CHUNK
    half = n_ch // 2
    cols = out.shape[1]
    me = lax.axis_index("seq")
    mc = lax.axis_index("ch")
    strand_me = mc // half

    barrier = pltpu.get_barrier_semaphore()
    for d in range(1, n_seq):
        pl.semaphore_signal(
            barrier, inc=1, device_id={"seq": lax.rem(me + d, n_seq), "ch": mc}, device_id_type=MESH
        )
    for d in range(1, n_ch):
        pl.semaphore_signal(
            barrier, inc=1, device_id={"seq": me, "ch": lax.rem(mc + d, n_ch)}, device_id_type=MESH
        )
    pl.semaphore_wait(barrier, n_seq + n_ch - 2)

    right = lax.rem(me + 1, n_seq)
    left = lax.rem(me + n_seq - 1, n_seq)
    to_right = pltpu.make_async_remote_copy(
        src_ref=hid.at[pl.ds(rows - HALO, HALO)], dst_ref=halo_lo,
        send_sem=h_send.at[0], recv_sem=h_recv.at[0],
        device_id={"seq": right, "ch": mc}, device_id_type=MESH,
    )
    to_left = pltpu.make_async_remote_copy(
        src_ref=hid.at[pl.ds(0, HALO)], dst_ref=halo_hi,
        send_sem=h_send.at[1], recv_sem=h_recv.at[1],
        device_id={"seq": left, "ch": mc}, device_id_type=MESH,
    )
    to_right.start()
    to_left.start()

    def column_block(owner):
        return owner + (owner // half) * (n_ch - 1 - 2 * owner)

    def w_copy(target):
        at = pl.multiple_of(column_block(target) * cols, cols)
        return pltpu.make_async_remote_copy(
            src_ref=outp.at[:, pl.ds(at, cols)], dst_ref=wout.at[mc],
            send_sem=w_send.at[target], recv_sem=w_recv.at[mc],
            device_id={"seq": me, "ch": target}, device_id_type=MESH,
        )

    for d in range(1, n_ch):
        w_copy(lax.rem(mc + d, n_ch)).start()
    wout[mc] = outp[:, pl.ds(pl.multiple_of(column_block(mc) * cols, cols), cols)]

    flip = reversal(width)
    big = 256 if rows % 256 == 0 else CHUNK
    bias = par[0:1, :]
    rate = par[1:2, :]
    skip = par[2:3, :]
    gain = par[3:4, :]

    def strand_rows(ref, s, at, count):
        u = ref[pl.ds(at, count), pl.ds(s * width, width)]
        return u if s == 0 else mm(u, flip).astype(BF16)

    for s in range(2):
        @pl.loop(0, rows // big)
        def _(k):
            at = pl.multiple_of(k * big, big)
            p = mm(strand_rows(hid, s, at, big), wts[...])
            z = p[:, :inner].astype(BF16).astype(F32)
            gate[s, pl.ds(at, big), :] = silu(z)
            xbc[s, pl.ds(pl.multiple_of(HALO + at, HALO), big), :] = (
                p[:, inner : inner + conv].astype(BF16).astype(F32)
            )
            v = p[:, inner + conv :] + bias
            step[s, pl.ds(at, big), :] = jnp.maximum(v, 0.0) + jnp.log1p(jnp.exp(-jnp.abs(v)))

    to_right.wait_recv()
    to_left.wait_recv()
    for s in range(2):
        wc = wts[:, inner : inner + conv]
        lo = mm(strand_rows(halo_lo, s, 0, HALO), wc).astype(BF16).astype(F32)
        hi = mm(strand_rows(halo_hi, s, 0, HALO), wc).astype(BF16).astype(F32)
        xbc[s, 0:HALO, :] = jnp.where(me > 0, lo, 0.0)
        xbc[s, rows + HALO : rows + 2 * HALO, :] = jnp.where(me < n_seq - 1, hi, 0.0)

    row_i = lax.broadcasted_iota(jnp.int32, (CHUNK, CHUNK), 0)
    col_i = lax.broadcasted_iota(jnp.int32, (CHUNK, CHUNK), 1)
    tri = jnp.where(row_i >= col_i, 1.0, 0.0).astype(BF16)

    @pl.loop(0, 2 * chunks)
    def _(k):
        s = k // chunks
        c = k % chunks
        at = pl.multiple_of(c * CHUNK, CHUNK)
        dt = step[s, pl.ds(at, CHUNK), :]
        ld = -dt * rate
        ld_hi = ld.astype(BF16)
        rest = ld - ld_hi.astype(F32)
        ld_mid = rest.astype(BF16)
        ld_lo = (rest - ld_mid.astype(F32)).astype(BF16)
        ahead = mm(tri, ld_hi) + (mm(tri, ld_mid) + mm(tri, ld_lo))
        total = ahead[CHUNK - 1 :, :]
        behind = total - ahead + ld
        cum[s, 0, pl.ds(at, CHUNK), :] = ahead
        cum[s, 1, pl.ds(at, CHUNK), :] = behind
        tot[s, c] = jnp.broadcast_to(total, (8, inner))
        window = xbc[s, pl.ds(pl.multiple_of(at + HALO - 8, 8), CHUNK + 16), :]
        for d in range(2):
            acc = None
            for j in range(taps_count):
                off = j - (taps_count - 1) if d == 0 else taps_count - 1 - j
                term = taps[j : j + 1, :] * window[8 + off : 8 + off + CHUNK, :]
                acc = term if acc is None else acc + term
            act = silu(acc)
            act16 = act.astype(BF16)
            xs[s, d, pl.ds(at, CHUNK), :] = act16[:, :inner]
            bc[s, d, pl.ds(at, CHUNK), :] = act16[:, inner:]
            weighted = act16[:, :inner].astype(F32) * dt
            xdt[s, d, pl.ds(at, CHUNK), :] = weighted.astype(BF16)
            left_over = total - (ahead if d == 0 else behind)
            loaded = (weighted * jnp.exp(left_over)).astype(BF16)
            b_t = act[:, inner:].T[:state].astype(BF16)
            sadd[s, d, c] = mm(b_t, loaded)

    for s in range(2):
        whole = tot[s, 0, 0:1, :]
        for c in range(1, chunks):
            whole = whole + tot[s, c, 0:1, :]
        tt_out[s : s + 1, :] = whole
        for d in range(2):
            carry = jnp.zeros((state, inner), F32)
            for k in range(chunks):
                c = k if d == 0 else chunks - 1 - k
                sent[s, d, c] = carry
                carry = jnp.exp(tot[s, c, 0:1, :]) * carry + sadd[s, d, c]
            st_out[d, s * state : (s + 1) * state, :] = carry.astype(BF16)

    def t_copy(target):
        return pltpu.make_async_remote_copy(
            src_ref=tt_out, dst_ref=tt_in.at[me],
            send_sem=t_send.at[target], recv_sem=t_recv.at[me],
            device_id={"seq": target, "ch": mc}, device_id_type=MESH,
        )

    def s_copy(target):
        earlier = (n_seq + me - target) // n_seq
        return pltpu.make_async_remote_copy(
            src_ref=st_out.at[earlier], dst_ref=st_in.at[me],
            send_sem=s_send.at[target], recv_sem=s_recv.at[me],
            device_id={"seq": target, "ch": mc}, device_id_type=MESH,
        )

    for d in range(1, n_seq):
        target = lax.rem(me + d, n_seq)
        t_copy(target).start()
        s_copy(target).start()

    lane = lax.broadcasted_iota(jnp.int32, (CHUNK, inner), 1)
    pair = lax.broadcasted_iota(jnp.int32, (CHUNK, 128), 1)
    first = lax.rem(pair, hp) < hp // 2

    @pl.loop(0, 2 * chunks)
    def _(k):
        s = k // chunks
        c = k % chunks
        at = pl.multiple_of(c * CHUNK, CHUNK)
        both = [cum[s, d, pl.ds(at, CHUNK), :] for d in range(2)]
        turned = [
            jnp.where(first, both[0][:, q : q + 128], both[1][:, q : q + 128]).T
            for q in range(0, inner, 128)
        ]
        for d in range(2):
            maps = bc[s, d, pl.ds(at, CHUNK), :]
            scores = mm_nt(maps[:, state:], maps[:, :state])
            keep = row_i >= col_i if d == 0 else row_i <= col_i
            parts = []
            for h in range(heads):
                q = h * hp
                column = both[d][:, q : q + 1]
                r = q % 128 + d * (hp // 2)
                across = turned[q // 128][r : r + 1, :]
                decay = jnp.exp(jnp.where(keep, column - across, -1e30))
                parts.append((scores * decay).astype(BF16))
            weights = jnp.concatenate(parts, axis=1)
            moved = xdt[s, d, pl.ds(at, CHUNK), :]
            zero = jnp.zeros_like(moved)
            diagonal = jnp.concatenate(
                [jnp.where(lane // hp == h, moved, zero) for h in range(heads)], axis=0
            )
            y[s, d, pl.ds(at, CHUNK), :] = mm(weights, diagonal) + skip * xs[
                s, d, pl.ds(at, CHUNK), :
            ].astype(F32)

    for d in range(1, n_ch):
        w_copy(lax.rem(mc + n_ch - d, n_ch)).wait_send()
    flip_out = reversal(cols)
    for i in range(n_ch):
        @pl.when(mc != i)
        def _():
            pltpu.make_async_remote_copy(
                src_ref=outp.at[:, pl.ds(0, cols)], dst_ref=wout.at[i],
                send_sem=w_send.at[i], recv_sem=w_recv.at[i],
                device_id={"seq": me, "ch": i}, device_id_type=MESH,
            ).wait_recv()
        plain = wout[i]
        wrev[i] = jnp.where(strand_me > 0, mm(plain, flip_out).astype(BF16), plain)

    def arrive(i):
        pltpu.make_async_remote_copy(
            src_ref=tt_out, dst_ref=tt_in.at[i], send_sem=t_send.at[i], recv_sem=t_recv.at[i],
            device_id={"seq": i, "ch": mc}, device_id_type=MESH,
        ).wait_recv()
        pltpu.make_async_remote_copy(
            src_ref=st_out.at[0], dst_ref=st_in.at[i], send_sem=s_send.at[i],
            recv_sem=s_recv.at[i], device_id={"seq": i, "ch": mc}, device_id_type=MESH,
        ).wait_recv()

    def absorb(i, carry):
        arrive(i)
        grown = []
        for s in range(2):
            grown.append(
                jnp.exp(tt_in[i, s : s + 1, :]) * carry[s]
                + st_in[i, s * state : (s + 1) * state, :].astype(F32)
            )
        return tuple(grown)

    nothing = jnp.zeros((state, inner), F32)
    rising = lax.fori_loop(0, me, absorb, (nothing, nothing))
    falling = lax.fori_loop(
        0, n_seq - 1 - me, lambda k, carry: absorb(n_seq - 1 - k, carry), (nothing, nothing)
    )
    for s in range(2):
        for d in range(2):
            carry = rising[s] if d == 0 else falling[s]
            for k in range(chunks):
                c = k if d == 0 else chunks - 1 - k
                sfin[s, d, c] = (sent[s, d, c] + carry).astype(BF16)
                carry = jnp.exp(tot[s, c, 0:1, :]) * carry

    group_r = lax.broadcasted_iota(jnp.int32, (inner, inner), 0) // hp
    group_c = lax.broadcasted_iota(jnp.int32, (inner, inner), 1) // hp
    mean_of = jnp.where(group_r == group_c, 1.0 / hp, 0.0).astype(BF16)

    def m_copy(s, c, target):
        at = pl.multiple_of(c * CHUNK, CHUNK)
        return pltpu.make_async_remote_copy(
            src_ref=mixed.at[s, pl.ds(at, CHUNK)],
            dst_ref=gath.at[mc, pl.ds(at, CHUNK)],
            send_sem=m_send.at[target, c], recv_sem=m_recv.at[mc, c],
            device_id={"seq": me, "ch": target}, device_id_type=MESH,
        )

    def mix(s, c):
        at = pl.multiple_of(c * CHUNK, CHUNK)
        z = gate[s, pl.ds(at, CHUNK), :]
        result = None
        for d in range(2):
            carried = mm(bc[s, d, pl.ds(at, CHUNK), :][:, state:], sfin[s, d, c])
            full = y[s, d, pl.ds(at, CHUNK), :] + jnp.exp(cum[s, d, pl.ds(at, CHUNK), :]) * carried
            gated = full * z
            square = mm((gated * gated).astype(BF16), mean_of)
            normed = gated * lax.rsqrt(square + EPS)
            result = normed if result is None else result + normed
        return (result * gain).astype(BF16)

    other = 1 - strand_me

    @pl.loop(0, chunks)
    def _(c):
        mixed[other, pl.ds(pl.multiple_of(c * CHUNK, CHUNK), CHUNK), :] = mix(other, c)
        for j in range(half):
            m_copy(other, c, other * half + j).start()

    @pl.loop(0, chunks)
    def _(c):
        at = pl.multiple_of(c * CHUNK, CHUNK)
        value = mix(strand_me, c)
        mixed[strand_me, pl.ds(at, CHUNK), :] = value
        gath[mc, pl.ds(at, CHUNK), :] = value
        for j in range(1, half):
            m_copy(strand_me, c, strand_me * half + lax.rem(mc + j, half)).start()

    @pl.loop(0, chunks)
    def _(c):
        at = pl.multiple_of(c * CHUNK, CHUNK)
        for d in range(1, n_ch):
            source = lax.rem(mc + d, n_ch)
            pltpu.make_async_remote_copy(
                src_ref=mixed.at[0, pl.ds(at, CHUNK)],
                dst_ref=gath.at[source, pl.ds(at, CHUNK)],
                send_sem=m_send.at[source, c], recv_sem=m_recv.at[source, c],
                device_id={"seq": me, "ch": source}, device_id_type=MESH,
            ).wait_recv()
        total = hid[pl.ds(at, CHUNK), pl.ds(pl.multiple_of(mc * cols, cols), cols)].astype(F32)
        branch = mm(gath[0, pl.ds(at, CHUNK), :], wrev[0])
        for i in range(1, n_ch):
            branch = branch + mm(gath[i, pl.ds(at, CHUNK), :], wrev[i])
        out[pl.ds(at, CHUNK), :] = (total + branch).astype(BF16)

    to_right.wait_send()
    to_left.wait_send()
    for d in range(1, n_seq):
        target = lax.rem(me + d, n_seq)
        t_copy(target).wait_send()
        s_copy(target).wait_send()

    @pl.loop(0, chunks)
    def _(c):
        for j in range(half):
            m_copy(other, c, other * half + j).wait_send()
        for j in range(1, half):
            m_copy(strand_me, c, strand_me * half + lax.rem(mc + j, half)).wait_send()


def shards(
    n_seq, n_ch,
    hidden_in, proj_zx, proj_bc, proj_dt, conv_x, conv_bc,
    dt_bias, decay_exp, skip_gain, norm_gain, out_proj,
):
    rows = hidden_in.shape[0]
    width = hidden_in.shape[1] // 2
    inner = proj_zx.shape[2]
    heads = dt_bias.shape[0]
    hp = inner // heads
    bcw = proj_bc.shape[1]
    state = bcw // 2
    conv = inner + bcw
    chunks = rows // CHUNK
    cols = hidden_in.shape[1] // n_ch
    wts = jnp.concatenate(
        [proj_zx.reshape(width, 2 * inner), proj_bc, jnp.repeat(proj_dt, hp, axis=1)], axis=1
    )
    taps = jnp.concatenate([conv_x, conv_bc], axis=1).astype(F32)
    rate = jnp.exp2(-decay_exp.astype(F32))
    per_head = jnp.repeat(jnp.stack([dt_bias, rate, skip_gain]), hp, axis=1)
    par = jnp.concatenate([per_head, norm_gain[None]], axis=0)
    dma = pltpu.SemaphoreType.DMA
    vm = pltpu.VMEM
    scratch = [
        vm((HALO, 2 * width), BF16), vm((HALO, 2 * width), BF16),
        vm((2, rows + 2 * HALO, conv), F32),
        vm((2, rows, inner), F32), vm((2, rows, inner), F32),
        vm((2, 2, rows, inner), BF16), vm((2, 2, rows, inner), BF16),
        vm((2, 2, rows, bcw), BF16),
        vm((2, 2, rows, inner), F32),
        vm((2, 2, chunks, state, inner), F32), vm((2, 2, chunks, state, inner), F32),
        vm((2, 2, chunks, state, inner), BF16),
        vm((2, chunks, 8, inner), F32),
        vm((2, 2, rows, inner), F32),
        vm((2, 2 * state, inner), BF16), vm((8, inner), F32),
        vm((n_seq, 2 * state, inner), BF16), vm((n_seq, 8, inner), F32),
        vm((n_ch, inner, cols), BF16), vm((n_ch, inner, cols), BF16),
        vm((2, rows, inner), BF16), vm((n_ch, rows, inner), BF16),
        dma((2,)), dma((2,)), dma((n_ch,)), dma((n_ch,)),
        dma((n_seq,)), dma((n_seq,)), dma((n_seq,)), dma((n_seq,)),
        dma((n_ch, chunks)), dma((n_ch, chunks)),
    ]
    return pl.pallas_call(
        functools.partial(kernel, n_seq, n_ch, heads, conv_x.shape[0]),
        out_shape=jax.ShapeDtypeStruct((rows, cols), BF16),
        in_specs=[pl.BlockSpec(memory_space=vm)] * 5,
        out_specs=pl.BlockSpec(memory_space=vm),
        scratch_shapes=scratch,
        compiler_params=pltpu.CompilerParams(
            collective_id=0, has_side_effects=True, vmem_limit_bytes=48 * 1024 * 1024
        ),
    )(hidden_in, wts, taps, par, out_proj)


def solution(mesh):
    n_seq, n_ch = mesh.shape["seq"], mesh.shape["ch"]
    placed = (
        P("seq", None),
        P(None, None, "ch"),
        P(),
        P(None, "ch"),
        P(None, "ch"),
        P(),
        P("ch"),
        P("ch"),
        P("ch"),
        P("ch"),
        P("ch", None),
    )
    return jax.shard_map(
        functools.partial(shards, n_seq, n_ch),
        mesh=mesh, in_specs=placed, out_specs=P("seq", "ch"), check_vma=False,
    )
```

```python
import functools

import jax
import jax.numpy as jnp
from jax import lax
from jax.experimental import pallas as pl
from jax.experimental.pallas import tpu as pltpu
from jax.sharding import PartitionSpec as P

EPS = 1e-05
CHUNK = 128
HALO = 16
F32 = jnp.float32
BF16 = jnp.bfloat16
MESH = pl.DeviceIdType.MESH


def mm(a, b):
    return jnp.dot(a, b, preferred_element_type=F32)


def mm_nt(a, b):
    return lax.dot_general(a, b, (((1,), (1,)), ((), ())), preferred_element_type=F32)


def silu(v):
    half = 0.5 * v
    return half + half * jnp.tanh(half)


def reversal(size):
    row = lax.broadcasted_iota(jnp.int32, (size, size), 0)
    col = lax.broadcasted_iota(jnp.int32, (size, size), 1)
    return jnp.where(row + col == size - 1, 1.0, 0.0).astype(BF16)


def kernel(
    n_seq, n_ch, heads, taps_count,
    hid, wts, taps, par, outp, out,
    halo_lo, halo_hi, xbc, gate, step, xs, xdt, bc, cum, sadd, sent, sfin, tot, y,
    st_out, tt_out, st_in, tt_in, wout, wrev, mixed, gath,
    h_send, h_recv, w_send, w_recv, s_send, s_recv, t_send, t_recv, m_send, m_recv, r_send,
):
    rows, two_width = hid.shape
    width = two_width // 2
    inner = par.shape[1]
    bcw = wts.shape[1] - 3 * inner
    state = bcw // 2
    hp = inner // heads
    conv = inner + bcw
    chunks = rows // CHUNK
    half = n_ch // 2
    cols = out.shape[1]
    me = lax.axis_index("seq")
    mc = lax.axis_index("ch")
    strand_me = mc // half
    other = 1 - strand_me
    local = lax.rem(mc, half)

    barrier = pltpu.get_barrier_semaphore()
    for d in range(1, n_seq):
        pl.semaphore_signal(
            barrier, inc=1, device_id={"seq": lax.rem(me + d, n_seq), "ch": mc}, device_id_type=MESH
        )
    for d in range(1, n_ch):
        pl.semaphore_signal(
            barrier, inc=1, device_id={"seq": me, "ch": lax.rem(mc + d, n_ch)}, device_id_type=MESH
        )
    pl.semaphore_wait(barrier, n_seq + n_ch - 2)

    right = lax.rem(me + 1, n_seq)
    left = lax.rem(me + n_seq - 1, n_seq)
    to_right = pltpu.make_async_remote_copy(
        src_ref=hid.at[pl.ds(rows - HALO, HALO)], dst_ref=halo_lo,
        send_sem=h_send.at[0], recv_sem=h_recv.at[0],
        device_id={"seq": right, "ch": mc}, device_id_type=MESH,
    )
    to_left = pltpu.make_async_remote_copy(
        src_ref=hid.at[pl.ds(0, HALO)], dst_ref=halo_hi,
        send_sem=h_send.at[1], recv_sem=h_recv.at[1],
        device_id={"seq": left, "ch": mc}, device_id_type=MESH,
    )
    @pl.when(me < n_seq - 1)
    def _():
        to_right.start()

    @pl.when(me > 0)
    def _():
        to_left.start()


    def column_block(owner):
        return owner + (owner // half) * (n_ch - 1 - 2 * owner)

    def w_copy(target):
        at = pl.multiple_of(column_block(target) * cols, cols)
        return pltpu.make_async_remote_copy(
            src_ref=outp.at[:, pl.ds(at, cols)], dst_ref=wout.at[mc],
            send_sem=w_send.at[target], recv_sem=w_recv.at[mc],
            device_id={"seq": me, "ch": target}, device_id_type=MESH,
        )

    for d in range(1, n_ch):
        w_copy(lax.rem(mc + d, n_ch)).start()
    wout[mc] = outp[:, pl.ds(pl.multiple_of(column_block(mc) * cols, cols), cols)]

    flip = reversal(width)
    big = 256 if rows % 256 == 0 else CHUNK
    bias = par[0:1, :]
    rate = par[1:2, :]
    skip = par[2:3, :]
    gain = par[3:4, :]

    def strand_rows(ref, s, at, count):
        u = ref[pl.ds(at, count), pl.ds(s * width, width)]
        return u if s == 0 else mm(u, flip).astype(BF16)

    def project(s):
        @pl.loop(0, rows // big)
        def _(k):
            at = pl.multiple_of(k * big, big)
            p = mm(strand_rows(hid, s, at, big), wts[...])
            z = p[:, :inner].astype(BF16).astype(F32)
            gate[s, pl.ds(at, big), :] = silu(z)
            xbc[s, pl.ds(pl.multiple_of(HALO + at, HALO), big), :] = (
                p[:, inner : inner + conv].astype(BF16).astype(F32)
            )
            v = p[:, inner + conv :] + bias
            step[s, pl.ds(at, big), :] = jnp.maximum(v, 0.0) + jnp.log1p(jnp.exp(-jnp.abs(v)))

    def project_strand(which):
        for s in range(2):
            @pl.when(which == s)
            def _():
                project(s)

    def project_halo():
      @pl.when(me > 0)
      def _():
        to_right.wait_recv()

      @pl.when(me < n_seq - 1)
      def _():
        to_left.wait_recv()

      for s in range(2):
        wc = wts[:, inner : inner + conv]
        lo = mm(strand_rows(halo_lo, s, 0, HALO), wc).astype(BF16).astype(F32)
        hi = mm(strand_rows(halo_hi, s, 0, HALO), wc).astype(BF16).astype(F32)
        xbc[s, 0:HALO, :] = jnp.where(me > 0, lo, 0.0)
        xbc[s, rows + HALO : rows + 2 * HALO, :] = jnp.where(me < n_seq - 1, hi, 0.0)

    row_i = lax.broadcasted_iota(jnp.int32, (CHUNK, CHUNK), 0)
    col_i = lax.broadcasted_iota(jnp.int32, (CHUNK, CHUNK), 1)
    tri = jnp.where(row_i >= col_i, 1.0, 0.0).astype(BF16)

    def scan_block(s, c):
        at = pl.multiple_of(c * CHUNK, CHUNK)
        dt = step[s, pl.ds(at, CHUNK), :]
        ld = -dt * rate
        ld_hi = ld.astype(BF16)
        rest = ld - ld_hi.astype(F32)
        ld_mid = rest.astype(BF16)
        ld_lo = (rest - ld_mid.astype(F32)).astype(BF16)
        ahead = mm(tri, ld_hi) + (mm(tri, ld_mid) + mm(tri, ld_lo))
        total = ahead[CHUNK - 1 :, :]
        behind = total - ahead + ld
        cum[s, 0, pl.ds(at, CHUNK), :] = ahead
        cum[s, 1, pl.ds(at, CHUNK), :] = behind
        tot[s, c] = jnp.broadcast_to(total, (8, inner))
        window = xbc[s, pl.ds(pl.multiple_of(at + HALO - 8, 8), CHUNK + 16), :]
        for d in range(2):
            acc = None
            for j in range(taps_count):
                off = j - (taps_count - 1) if d == 0 else taps_count - 1 - j
                term = taps[j : j + 1, :] * window[8 + off : 8 + off + CHUNK, :]
                acc = term if acc is None else acc + term
            act = silu(acc)
            act16 = act.astype(BF16)
            xs[s, d, pl.ds(at, CHUNK), :] = act16[:, :inner]
            bc[s, d, pl.ds(at, CHUNK), :] = act16[:, inner:]
            weighted = act16[:, :inner].astype(F32) * dt
            xdt[s, d, pl.ds(at, CHUNK), :] = weighted.astype(BF16)
            left_over = total - (ahead if d == 0 else behind)
            loaded = (weighted * jnp.exp(left_over)).astype(BF16)
            b_t = act[:, inner:].T[:state].astype(BF16)
            sadd[s, d, c] = mm(b_t, loaded)

    def local_states(s):
        whole = tot[s, 0, 0:1, :]
        for c in range(1, chunks):
            whole = whole + tot[s, c, 0:1, :]
        tt_out[s] = jnp.broadcast_to(whole, (8, inner))
        for d in range(2):
            carry = jnp.zeros((state, inner), F32)
            for k in range(chunks):
                c = k if d == 0 else chunks - 1 - k
                sent[s, d, c] = carry
                carry = jnp.exp(tot[s, c, 0:1, :]) * carry + sadd[s, d, c]
            st_out[s, d] = carry.astype(BF16)

    def t_copy(s, target):
        return pltpu.make_async_remote_copy(
            src_ref=tt_out.at[s], dst_ref=tt_in.at[s, me],
            send_sem=t_send.at[s, target], recv_sem=t_recv.at[s, me],
            device_id={"seq": target, "ch": mc}, device_id_type=MESH,
        )

    def s_copy(s, target):
        earlier = (n_seq + me - target) // n_seq
        return pltpu.make_async_remote_copy(
            src_ref=st_out.at[s, earlier], dst_ref=st_in.at[s, me],
            send_sem=s_send.at[s, target], recv_sem=s_recv.at[s, me],
            device_id={"seq": target, "ch": mc}, device_id_type=MESH,
        )

    def send_states(s):
        local_states(s)
        for d in range(1, n_seq):
            target = lax.rem(me + d, n_seq)
            t_copy(s, target).start()
            s_copy(s, target).start()

    project_strand(other)

    @pl.loop(1, chunks - 1)
    def _(c):
        scan_block(other, c)

    project_halo()

    @pl.loop(0, 2)
    def _(k):
        scan_block(other, k * (chunks - 1))

    send_states(other)
    project_strand(strand_me)

    @pl.loop(0, chunks)
    def _(c):
        scan_block(strand_me, c)

    send_states(strand_me)

    lane = lax.broadcasted_iota(jnp.int32, (CHUNK, inner), 1)
    pair = lax.broadcasted_iota(jnp.int32, (CHUNK, 128), 1)
    first = lax.rem(pair, hp) < hp // 2

    def within_block(s, c):
        at = pl.multiple_of(c * CHUNK, CHUNK)
        both = [cum[s, d, pl.ds(at, CHUNK), :] for d in range(2)]
        turned = [
            jnp.where(first, both[0][:, q : q + 128], both[1][:, q : q + 128]).T
            for q in range(0, inner, 128)
        ]
        for d in range(2):
            maps = bc[s, d, pl.ds(at, CHUNK), :]
            scores = mm_nt(maps[:, state:], maps[:, :state])
            keep = row_i >= col_i if d == 0 else row_i <= col_i
            parts = []
            for h in range(heads):
                q = h * hp
                column = both[d][:, q : q + 1]
                r = q % 128 + d * (hp // 2)
                across = turned[q // 128][r : r + 1, :]
                decay = jnp.exp(jnp.where(keep, column - across, -1e30))
                parts.append((scores * decay).astype(BF16))
            weights = jnp.concatenate(parts, axis=1)
            moved = xdt[s, d, pl.ds(at, CHUNK), :]
            zero = jnp.zeros_like(moved)
            diagonal = jnp.concatenate(
                [jnp.where(lane // hp == h, moved, zero) for h in range(heads)], axis=0
            )
            y[s, d, pl.ds(at, CHUNK), :] = mm(weights, diagonal) + skip * xs[
                s, d, pl.ds(at, CHUNK), :
            ].astype(F32)

    @pl.loop(0, chunks)
    def _(c):
        within_block(other, c)

    for d in range(1, n_ch):
        w_copy(lax.rem(mc + n_ch - d, n_ch)).wait_send()
    flip_out = reversal(cols)
    for i in range(n_ch):
        @pl.when(mc != i)
        def _():
            pltpu.make_async_remote_copy(
                src_ref=outp.at[:, pl.ds(0, cols)], dst_ref=wout.at[i],
                send_sem=w_send.at[i], recv_sem=w_recv.at[i],
                device_id={"seq": me, "ch": i}, device_id_type=MESH,
            ).wait_recv()
        plain = wout[i]
        wrev[i] = jnp.where(strand_me > 0, mm(plain, flip_out).astype(BF16), plain)

    def absorb(s, i, carry):
        pltpu.make_async_remote_copy(
            src_ref=tt_out.at[s], dst_ref=tt_in.at[s, i], send_sem=t_send.at[s, i],
            recv_sem=t_recv.at[s, i], device_id={"seq": i, "ch": mc}, device_id_type=MESH,
        ).wait_recv()
        pltpu.make_async_remote_copy(
            src_ref=st_out.at[s, 0], dst_ref=st_in.at[s, i], send_sem=s_send.at[s, i],
            recv_sem=s_recv.at[s, i], device_id={"seq": i, "ch": mc}, device_id_type=MESH,
        ).wait_recv()
        return jnp.exp(tt_in[s, i, 0:1, :]) * carry + st_in[s, i].astype(F32)

    def enter_states(s):
        nothing = jnp.zeros((state, inner), F32)
        rising = lax.fori_loop(0, me, lambda i, carry: absorb(s, i, carry), nothing)
        falling = lax.fori_loop(
            0, n_seq - 1 - me, lambda k, carry: absorb(s, n_seq - 1 - k, carry), nothing
        )
        for d in range(2):
            carry = rising if d == 0 else falling
            for k in range(chunks):
                c = k if d == 0 else chunks - 1 - k
                sfin[s, d, c] = (sent[s, d, c] + carry).astype(BF16)
                carry = jnp.exp(tot[s, c, 0:1, :]) * carry

    group_r = lax.broadcasted_iota(jnp.int32, (inner, inner), 0) // hp
    group_c = lax.broadcasted_iota(jnp.int32, (inner, inner), 1) // hp
    mean_of = jnp.where(group_r == group_c, 1.0 / hp, 0.0).astype(BF16)

    def m_copy(s, c, target):
        at = pl.multiple_of(c * CHUNK, CHUNK)
        return pltpu.make_async_remote_copy(
            src_ref=mixed.at[s, pl.ds(at, CHUNK)],
            dst_ref=gath.at[mc, pl.ds(at, CHUNK)],
            send_sem=m_send.at[target, c], recv_sem=m_recv.at[mc, c],
            device_id={"seq": me, "ch": target}, device_id_type=MESH,
        )

    def mix(s, c):
        at = pl.multiple_of(c * CHUNK, CHUNK)
        z = gate[s, pl.ds(at, CHUNK), :]
        result = None
        for d in range(2):
            carried = mm(bc[s, d, pl.ds(at, CHUNK), :][:, state:], sfin[s, d, c])
            full = y[s, d, pl.ds(at, CHUNK), :] + jnp.exp(cum[s, d, pl.ds(at, CHUNK), :]) * carried
            gated = full * z
            square = mm((gated * gated).astype(BF16), mean_of)
            normed = gated * lax.rsqrt(square + EPS)
            result = normed if result is None else result + normed
        return (result * gain).astype(BF16)

    def first_owner(c):
        return other * half + lax.rem(c, half)

    enter_states(other)

    @pl.loop(0, chunks)
    def _(c):
        mixed[other, pl.ds(pl.multiple_of(c * CHUNK, CHUNK), CHUNK), :] = mix(other, c)
        m_copy(other, c, first_owner(c)).start()

    @pl.loop(0, chunks)
    def _(c):
        within_block(strand_me, c)

    enter_states(strand_me)

    @pl.loop(0, chunks)
    def _(c):
        at = pl.multiple_of(c * CHUNK, CHUNK)
        value = mix(strand_me, c)
        mixed[strand_me, pl.ds(at, CHUNK), :] = value
        gath[mc, pl.ds(at, CHUNK), :] = value
        for j in range(1, half):
            m_copy(strand_me, c, strand_me * half + lax.rem(mc + j, half)).start()

    def arrive(source, c):
        at = pl.multiple_of(c * CHUNK, CHUNK)
        pltpu.make_async_remote_copy(
            src_ref=mixed.at[0, pl.ds(at, CHUNK)], dst_ref=gath.at[source, pl.ds(at, CHUNK)],
            send_sem=m_send.at[source, c], recv_sem=m_recv.at[source, c],
            device_id={"seq": me, "ch": lax.rem(mc + 1, n_ch)}, device_id_type=MESH,
        ).wait_recv()

    def relay(i, c, j):
        source = other * half + i
        at = pl.multiple_of(c * CHUNK, CHUNK)
        target = strand_me * half + lax.rem(mc + j, half)
        return pltpu.make_async_remote_copy(
            src_ref=gath.at[source, pl.ds(at, CHUNK)], dst_ref=gath.at[source, pl.ds(at, CHUNK)],
            send_sem=r_send.at[i * half + j, c], recv_sem=m_recv.at[source, c],
            device_id={"seq": me, "ch": target}, device_id_type=MESH,
        )

    @pl.loop(0, chunks // half)
    def _(k):
        c = k * half + local
        for i in range(half):
            arrive(other * half + i, c)
            for j in range(1, half):
                relay(i, c, j).start()

    @pl.loop(0, chunks)
    def _(c):
        at = pl.multiple_of(c * CHUNK, CHUNK)
        for j in range(1, half):
            arrive(strand_me * half + lax.rem(mc + j, half), c)

        @pl.when(lax.rem(c, half) != local)
        def _():
            for i in range(half):
                arrive(other * half + i, c)

        total = hid[pl.ds(at, CHUNK), pl.ds(pl.multiple_of(mc * cols, cols), cols)].astype(F32)
        branch = mm(gath[0, pl.ds(at, CHUNK), :], wrev[0])
        for i in range(1, n_ch):
            branch = branch + mm(gath[i, pl.ds(at, CHUNK), :], wrev[i])
        out[pl.ds(at, CHUNK), :] = (total + branch).astype(BF16)

    @pl.when(me < n_seq - 1)
    def _():
        to_right.wait_send()

    @pl.when(me > 0)
    def _():
        to_left.wait_send()

    for s in range(2):
        for d in range(1, n_seq):
            target = lax.rem(me + d, n_seq)
            t_copy(s, target).wait_send()
            s_copy(s, target).wait_send()

    @pl.loop(0, chunks)
    def _(c):
        m_copy(other, c, first_owner(c)).wait_send()
        for j in range(1, half):
            m_copy(strand_me, c, strand_me * half + lax.rem(mc + j, half)).wait_send()

    @pl.loop(0, chunks // half)
    def _(k):
        for i in range(half):
            for j in range(1, half):
                relay(i, k * half + local, j).wait_send()


def shards(
    n_seq, n_ch,
    hidden_in, proj_zx, proj_bc, proj_dt, conv_x, conv_bc,
    dt_bias, decay_exp, skip_gain, norm_gain, out_proj,
):
    rows = hidden_in.shape[0]
    width = hidden_in.shape[1] // 2
    inner = proj_zx.shape[2]
    heads = dt_bias.shape[0]
    hp = inner // heads
    bcw = proj_bc.shape[1]
    state = bcw // 2
    conv = inner + bcw
    chunks = rows // CHUNK
    half = n_ch // 2
    cols = hidden_in.shape[1] // n_ch
    wts = jnp.concatenate(
        [proj_zx.reshape(width, 2 * inner), proj_bc, jnp.repeat(proj_dt, hp, axis=1)], axis=1
    )
    taps = jnp.concatenate([conv_x, conv_bc], axis=1).astype(F32)
    rate = jnp.exp2(-decay_exp.astype(F32))
    per_head = jnp.repeat(jnp.stack([dt_bias, rate, skip_gain]), hp, axis=1)
    par = jnp.concatenate([per_head, norm_gain[None]], axis=0)
    dma = pltpu.SemaphoreType.DMA
    vm = pltpu.VMEM
    scratch = [
        vm((HALO, 2 * width), BF16), vm((HALO, 2 * width), BF16),
        vm((2, rows + 2 * HALO, conv), F32),
        vm((2, rows, inner), F32), vm((2, rows, inner), F32),
        vm((2, 2, rows, inner), BF16), vm((2, 2, rows, inner), BF16),
        vm((2, 2, rows, bcw), BF16),
        vm((2, 2, rows, inner), F32),
        vm((2, 2, chunks, state, inner), F32), vm((2, 2, chunks, state, inner), F32),
        vm((2, 2, chunks, state, inner), BF16),
        vm((2, chunks, 8, inner), F32),
        vm((2, 2, rows, inner), F32),
        vm((2, 2, state, inner), BF16), vm((2, 8, inner), F32),
        vm((2, n_seq, state, inner), BF16), vm((2, n_seq, 8, inner), F32),
        vm((n_ch, inner, cols), BF16), vm((n_ch, inner, cols), BF16),
        vm((2, rows, inner), BF16), vm((n_ch, rows, inner), BF16),
        dma((2,)), dma((2,)), dma((n_ch,)), dma((n_ch,)),
        dma((2, n_seq)), dma((2, n_seq)), dma((2, n_seq)), dma((2, n_seq)),
        dma((n_ch, chunks)), dma((n_ch, chunks)), dma((half * half, chunks)),
    ]
    return pl.pallas_call(
        functools.partial(kernel, n_seq, n_ch, heads, conv_x.shape[0]),
        out_shape=jax.ShapeDtypeStruct((rows, cols), BF16),
        in_specs=[pl.BlockSpec(memory_space=vm)] * 5,
        out_specs=pl.BlockSpec(memory_space=vm),
        scratch_shapes=scratch,
        compiler_params=pltpu.CompilerParams(
            collective_id=0, has_side_effects=True, vmem_limit_bytes=48 * 1024 * 1024
        ),
    )(hidden_in, wts, taps, par, out_proj)


def solution(mesh):
    n_seq, n_ch = mesh.shape["seq"], mesh.shape["ch"]
    placed = (
        P("seq", None),
        P(None, None, "ch"),
        P(),
        P(None, "ch"),
        P(None, "ch"),
        P(),
        P("ch"),
        P("ch"),
        P("ch"),
        P("ch"),
        P("ch", None),
    )
    return jax.shard_map(
        functools.partial(shards, n_seq, n_ch),
        mesh=mesh, in_specs=placed, out_specs=P("seq", "ch"), check_vma=False,
    )
```
